32 devices in a mesh: gx: 8 (over z, x), gy: 4 (over y, core).
Axes of the slice: x: 2, y: 2, z: 4, core: 2. Of those that a mesh axis runs over, the one named last changes fastest.
Arguments:
- fields: float32 [4, 32, 32, 512], P(None, 'gx', 'gy'), may hold values from -6 to 6
- velocity: float32 [3, 32, 32, 512], P(None, 'gx', 'gy'), may hold values from -4 to 4
- diffusion: float32 [4], replicated, may hold values from 0.1 to 0.6
- panel_owner: int32 [32768, 1], P(('gx', 'gy')), may hold values from 0 to 31; in each aligned block of 1024 rows (0 to 1023, 1024 to 2047, ...) at most 128 rows name the same one
- panel_cell: int32 [32768], P(('gx', 'gy')), may hold values from 0 to 16383
- panel_bins: int32 [16, 32768], P(None, ('gx', 'gy')), may hold values from 0 to 127
- panel_position: float32 [3, 32768], P(None, ('gx', 'gy')), may hold values from -1 to 1, as said below
- panel_area: float32 [32768], P(('gx', 'gy')), may hold values from 0.3 to 3
- observer_position: float32 [3, 2048], replicated, may hold values from -2 to 2.25, as said below
Outputs:
- advanced: float32 [4, 32, 32, 512], P(None, 'gx', 'gy')
- signal: float32 [2048, 128], P(('gx', 'gy'))
The draws below stay inside these ranges and needn't reach their ends.
Inputs may be any that keep to these rules, and one draw needn't show every extreme that they name: `panel_owner`: among the panels of one device at most 128 name the same brick, a bound that some block reaches; every brick is named somewhere. `panel_cell`: A cell of the owning brick, numbered (x * 8 + y) * 512 + z in that brick's own coordinates. `panel_position`: every panel's third coordinate is 0 or less. `observer_position`: every observer's third coordinate is 0.25 or more.
All inputs are finite; a program needn't handle non-finite values.
Results may differ from the reference program's by a relative error of at most 0.0029.
Values sent between devices are 32-bit elements; how exact they have to be, the bound alone decides.
A program may use at most 128 MiB of HBM per device.

```python
import math
import jax
import jax.numpy as jnp
import numpy as np
from jax import lax

BX = 4
BY = 8
BZ = 512
P_DEV = 1024
OBS = 2048
BINS = 128
OB = 128
NB = 16
NX = 32
NY = 32
PANELS = 32768
CAP = 128
N_GY = 4
DEVICES = 32


def draw_panel_position(key, part):
    across_key, height_key = jax.random.split(key)
    across = jax.random.uniform(across_key, (2, PANELS), jnp.float32, -1.0, 1.0)
    height = jax.random.uniform(height_key, (1, PANELS), jnp.float32, -1.0, 0.0)
    return jnp.concatenate([across, height], axis=0)


def draw_observer_position(key, part):
    across_key, height_key = jax.random.split(key)
    across = jax.random.uniform(across_key, (2, OBS), jnp.float32, -2.0, 2.0)
    height = jax.random.uniform(height_key, (1, OBS), jnp.float32, 0.25, 2.25)
    return jnp.concatenate([across, height], axis=0)


def plant(result, own_key, smallest, top_value):
    longest = result.shape.index(max(result.shape))
    spots = []
    for shift in (0, 1):
        where = [jax.random.randint(jax.random.fold_in(own_key, axis), (), 0, length) for axis, length in enumerate(result.shape)]
        where[longest] = (where[longest] + shift) % result.shape[longest]
        spots.append(tuple(where))
    return result.at[spots[0]].set(smallest).at[spots[1]].set(top_value)


def steps_of(stream_key, extent, cuts, least, high):
    gain = 1.0
    for dim, shards_of in cuts:
        steps = jax.random.uniform(jax.random.fold_in(jax.random.fold_in(stream_key, 6), dim), (shards_of,), jnp.float32, least / len(cuts), high / len(cuts))
        gain = gain * jnp.repeat(jnp.exp(steps), extent[dim] // shards_of).reshape((-1,) + (1,) * (len(extent) - 1 - dim))
    return gain


def routed_block(rng, own, number, rows, number_of, top, reach, lean):
    sequence = jax.random.permutation(rng, number_of)
    packed, common = shares(number_of, rows * top, reach, lean, True), shares(number_of, rows * top, reach, lean, False)
    places = jnp.arange(number_of)

    def named(lengths, turn):
        used = int((lengths > 0).sum())
        fixed = max(1, used // 4)
        shifted = fixed + (places - fixed + turn * (used - fixed)) % max(1, number_of - fixed)
        return jnp.zeros((number_of,), jnp.int32).at[sequence[jnp.where(places < fixed, places, shifted)]].set(jnp.asarray(lengths, jnp.int32))

    lengths = jnp.where(number % 4 == 0, named(packed, number // 4), named(common, number - number // 4 - 1))
    mixed = jax.random.permutation(jax.random.fold_in(own, 3), number_of)
    giver, receiver = mixed[0:number_of // 2 * 2:2], mixed[1:number_of // 2 * 2:2]
    slack = jnp.minimum(lengths[giver] - 1, reach - lengths[receiver]) // 2
    slack = jnp.where((giver == sequence[0]) | (receiver == sequence[0]) | (lengths[receiver] == 0), 0, jnp.maximum(slack, 0))
    shifted = jax.random.randint(jax.random.fold_in(own, 4), (number_of // 2,), 0, 1 << 20) % (slack + 1)
    lengths = lengths.at[giver].add(-shifted).at[receiver].add(shifted)
    items = jnp.searchsorted(jnp.cumsum(lengths), jnp.arange(rows * top), side="right").astype(jnp.int32)
    listing = items.reshape(top, rows).T
    listing = listing[jax.random.permutation(jax.random.fold_in(own, 1), rows)]
    turn = jax.random.randint(jax.random.fold_in(own, 2), (rows, 1), 0, top)
    return jnp.take_along_axis(listing, (jnp.arange(top)[None, :] + turn) % top, axis=1)


def shares(amount, total, bound, lean, full):
    portions = [(1 << 20) // math.isqrt(rank ** lean) + 1 for rank in range(1, amount + 1)]
    largest = bound if full else min(bound, max(-(-total // amount), total * portions[0] // sum(portions)))
    least = 1 if total - largest >= amount - 1 else 0
    holding, rest = [largest] + [least] * (amount - 1), total - largest - least * (amount - 1)
    while rest > 0:
        candidates = [i for i in range(1, amount) if holding[i] < largest] or [i for i in range(1, amount) if holding[i] < bound]
        mass, left = sum([portions[i] for i in candidates]), rest
        for i in candidates:
            addition = min(bound - holding[i], max(1, left * portions[i] // mass), rest)
            holding[i] = holding[i] + addition
            rest = rest - addition
    return np.array(holding)


def centred(own_key, dims, scale, reach, cuts=(), held_as=jnp.bfloat16):
    entries = scale * jax.random.normal(own_key, dims, jnp.float32)
    if cuts:
        entries = entries * steps_of(own_key, dims, cuts, -0.22, 0.18)
    return jnp.clip(entries, -reach, reach).astype(held_as)


def setup_inputs(seed: int = 0) -> dict:
    key_of = jax.random.split(jax.random.key(seed), 10)
    fields = centred(key_of[0], (4, NX, NY, BZ), 1.0, 6.0, ((1, 8), (2, 4)), jnp.float32)
    velocity = centred(key_of[1], (3, NX, NY, BZ), 1.0, 4.0, ((1, 8), (2, 4)), jnp.float32)
    diffusion = jnp.clip(jnp.exp(jax.random.uniform(key_of[2], (4,), jnp.float32, math.log(0.1), math.log(0.6))), 0.1, 0.6)
    panel_owner_keys = jax.random.split(jax.random.fold_in(key_of[3], 1), PANELS // P_DEV)
    panel_owner_turns = jax.random.permutation(jax.random.fold_in(key_of[3], 3), PANELS // P_DEV)
    panel_owner = jax.vmap(lambda own, number: routed_block(jax.random.fold_in(key_of[3], 2), own, number, P_DEV, DEVICES, 1, CAP, 2))(panel_owner_keys, panel_owner_turns).reshape((PANELS, 1))
    panel_cell = plant(jax.random.randint(key_of[4], (PANELS,), 0, BX * BY * BZ), jax.random.fold_in(key_of[4], 1), 0, (BX * BY * BZ) - 1).astype(jnp.int32)
    panel_bins = plant(jax.random.randint(key_of[5], (NB, PANELS), 0, BINS), jax.random.fold_in(key_of[5], 1), 0, BINS - 1).astype(jnp.int32)
    panel_position = draw_panel_position(jax.random.fold_in(key_of[9], 71), 0)
    panel_area = jnp.clip(jnp.exp(math.log(3.0) - 2.3025851 * jax.random.uniform(key_of[7], (PANELS,), jnp.float32) ** steps_of(key_of[7], (PANELS,), ((0, 32),), -0.2, 0.2)), 0.3, 3.0)
    observer_position = draw_observer_position(jax.random.fold_in(key_of[9], 71), 0)
    return {"fields": fields, "velocity": velocity, "diffusion": diffusion, "panel_owner": panel_owner, "panel_cell": panel_cell, "panel_bins": panel_bins, "panel_position": panel_position, "panel_area": panel_area, "observer_position": observer_position}


time_step = 0.15

def axis_terms(center, ahead_one, ahead_two, behind_one, behind_two):
    first = (8.0 * (ahead_one - behind_one) - (ahead_two - behind_two)) / 12.0
    second = (16.0 * (ahead_one + behind_one) - (ahead_two + behind_two) - 30.0 * center) / 12.0
    return (first, second)

def rates(padded, velocity, diffusion):
    center = padded[:, 2:-2, 2:-2, :]
    first_x, second_x = axis_terms(center, padded[:, 3:-1, 2:-2, :], padded[:, 4:, 2:-2, :], padded[:, 1:-3, 2:-2, :], padded[:, :-4, 2:-2, :])
    first_y, second_y = axis_terms(center, padded[:, 2:-2, 3:-1, :], padded[:, 2:-2, 4:, :], padded[:, 2:-2, 1:-3, :], padded[:, 2:-2, :-4, :])
    first_z, second_z = axis_terms(center, jnp.roll(center, -1, axis=3), jnp.roll(center, -2, axis=3), jnp.roll(center, 1, axis=3), jnp.roll(center, 2, axis=3))
    advect = velocity[0][None] * first_x + velocity[1][None] * first_y + velocity[2][None] * first_z
    return -advect + diffusion[:, None, None, None] * (second_x + second_y + second_z)

def wrap_pad(values):
    return jnp.pad(values, ((0, 0), (2, 2), (2, 2), (0, 0)), mode='wrap')

def emission(samples, position, area, bins_block, observers, scale):
    delta = observers[:, None, :] - position[:, :, None]
    inverse = lax.rsqrt(lax.optimization_barrier(jnp.sum(delta * delta, axis=0)))
    along = samples[1][:, None] * delta[0] + samples[2][:, None] * delta[1] + samples[3][:, None] * delta[2]
    emitted = scale * area[:, None] * (samples[0][:, None] + along * inverse) * inverse
    return emitted.astype(jnp.bfloat16)

def reference(fields, velocity, diffusion, panel_owner, panel_cell, panel_bins, panel_position, panel_area, observer_position):
    middle = fields + time_step * rates(wrap_pad(fields), velocity, diffusion)
    advanced = 0.5 * fields + 0.5 * (middle + time_step * rates(wrap_pad(middle), velocity, diffusion))
    owner = panel_owner[:, 0]
    brick_x = owner // N_GY
    brick_y = owner % N_GY
    local_x = panel_cell // (BY * BZ)
    local_y = panel_cell // BZ % BY
    local_z = panel_cell % BZ
    samples = fields[:, brick_x * BX + local_x, brick_y * BY + local_y, local_z]
    scale = (BINS / PANELS) ** 0.5
    sample_blocks = samples.reshape(4, DEVICES, P_DEV).transpose(1, 0, 2)
    position_blocks = panel_position.reshape(3, DEVICES, P_DEV).transpose(1, 0, 2)
    area_blocks = panel_area.reshape(DEVICES, P_DEV)
    bin_blocks = panel_bins.reshape(NB, DEVICES, P_DEV).transpose(1, 0, 2)
    levels = jnp.arange(BINS, dtype=jnp.int32)

    def accumulate(total, pieces):
        sample_block, position_block, area_block, bins_block = pieces
        emitted = emission(sample_block, position_block, area_block, bins_block, observer_position, scale)
        shaped = emitted.reshape(P_DEV, NB, OB).astype(jnp.float32)
        onehot = (bins_block[:, :, None] == levels[None, None, :]).astype(jnp.float32)
        return (total + jnp.einsum('pbo,bpt->bot', shaped, onehot), None)
    start = jnp.zeros((NB, OB, BINS), jnp.float32)
    total, unused = lax.scan(accumulate, start, (sample_blocks, position_blocks, area_blocks, bin_blocks))
    return (advanced, total.reshape(OBS, BINS))
```

```python
import functools

import jax
import jax.numpy as jnp
from jax import lax
from jax.experimental import pallas as pl
from jax.experimental.pallas import tpu as pltpu
from jax.sharding import PartitionSpec as P

MESH = pl.DeviceIdType.MESH
time_step = 0.15
NT = (((1,), (1,)), ((), ()))


def axis_terms(center, ahead_one, ahead_two, behind_one, behind_two):
    first = (8.0 * (ahead_one - behind_one) - (ahead_two - behind_two)) / 12.0
    second = (16.0 * (ahead_one + behind_one) - (ahead_two + behind_two) - 30.0 * center) / 12.0
    return (first, second)


def section(cells_ref, x_ref, y_ref, pad_ref, velocity_ref, diffusion_ref, write):
    quantities, nx, ny, nz = cells_ref.shape
    for c in range(quantities):
        def plane(x):
            if x < 0:
                return x_ref[0, c, 2 + x]
            if x >= nx:
                return x_ref[1, c, x - nx]
            return cells_ref[c, x]

        for x in range(nx):
            center = cells_ref[c, x]
            pad_ref[c, x, 6:8, :] = y_ref[0, c, x]
            pad_ref[c, x, 8:8 + ny, :] = center
            pad_ref[c, x, 8 + ny:10 + ny, :] = y_ref[1, c, x]

            def along_y(k):
                return pad_ref[c, x, 8 + k:8 + k + ny, :]

            first_x, second_x = axis_terms(
                center, plane(x + 1), plane(x + 2), plane(x - 1), plane(x - 2))
            first_y, second_y = axis_terms(
                center, along_y(1), along_y(2), along_y(-1), along_y(-2))
            first_z, second_z = axis_terms(
                center, pltpu.roll(center, nz - 1, 1), pltpu.roll(center, nz - 2, 1),
                pltpu.roll(center, 1, 1), pltpu.roll(center, 2, 1))
            advect = (
                velocity_ref[0, x] * first_x + velocity_ref[1, x] * first_y
                + velocity_ref[2, x] * first_z)
            write(c, x, center, -advect + diffusion_ref[c] * (second_x + second_y + second_z))


def two_parts(values, axis):
    high = values.astype(jnp.bfloat16)
    low = (values - high.astype(jnp.float32)).astype(jnp.bfloat16)
    return jnp.concatenate([high, low], axis=axis)


def three_parts(values):
    high = values.astype(jnp.bfloat16).astype(jnp.float32)
    rest = values - high
    middle = rest.astype(jnp.bfloat16).astype(jnp.float32)
    return high, middle, rest - middle


def observer_side(values, width):
    high, middle, low = three_parts(values)
    pieces = [high, middle, low, high, middle, high]
    used = len(pieces) * values.shape[0]
    filled = jnp.concatenate(pieces + [jnp.zeros((128 - used, width), jnp.float32)], axis=0)
    return filled.T.astype(jnp.bfloat16)


def panel_side(values):
    high, middle, low = three_parts(values)
    return jnp.concatenate([high, high, high, middle, middle, low], axis=0).astype(jnp.bfloat16)


def emission_kernel(
    grid_x, grid_y, cap, scale, tile,
    fields_in, velocity_in, diffusion_in, owner_in, cell_in, bins_in, position_in, area_in, observer_in,
    advanced_ref, signal_ref,
    fields_ref, velocity_ref, diffusion_ref, owner_ref, cell_ref, bins_ref, position_ref, area_ref, observer_ref,
    middle_ref, pad_ref, x_one_ref, x_two_ref, y_one_ref, y_two_ref, y_out_one_ref, y_out_two_ref,
    request_ref, arrived_ref, looked_ref, returned_ref, table_ref, ranked_ref,
    place_ref, lines_out_ref, lines_ref, weighted_ref, near_ref, toward_ref, inverse_ref, hot_ref, sum_ref, landed_ref,
    request_send, request_recv, sample_send, sample_recv, total_send, total_recv,
    halo_send, halo_recv, place_send, place_recv, lines_send, lines_recv, weighted_send, weighted_recv, load_sem,
):
    devices = grid_x * grid_y
    my_x, my_y = lax.axis_index("gx"), lax.axis_index("gy")
    me = my_x * grid_y + my_y
    nx, ny = fields_ref.shape[1:3]
    panels = owner_ref.shape[1]
    blocks, bins = bins_ref.shape[0], signal_ref.shape[1]
    observers = observer_ref.shape[1]
    width = observers // blocks
    share = observers // devices
    per_block = width // share
    quantities = fields_ref.shape[0]
    rows = fields_ref.shape[1] * fields_ref.shape[2]
    depth = fields_ref.shape[3]
    chunks = depth // 128
    row_shift = (depth - 1).bit_length()

    members = 2 * grid_y
    groups = devices // members
    own_blocks = blocks // members
    across = grid_y // 2
    my_bit = lax.rem(my_x // 2, 2)
    my_member = my_bit * grid_y + my_y
    my_group = (my_x // 4) * 2 + lax.rem(my_x, 2)

    def at(d):
        return (d // grid_y, lax.rem(d, grid_y))

    def member_at(group, member):
        x = (group // 2) * 4 + (member // grid_y) * 2 + lax.rem(group, 2)
        return (x, lax.rem(member, grid_y))

    def block_of(member, i):
        bit, y = member // grid_y, member % grid_y
        return ((y % 2) * 2 + bit) * (own_blocks * across) + i * across + y // 2

    def member_of(block):
        y = lax.rem(block, across)
        bit = lax.rem(block // (across * own_blocks), 2)
        core = block // (across * own_blocks * 2)
        return bit * grid_y + y * 2 + core

    barrier = pltpu.get_barrier_semaphore()

    @pl.loop(1, devices)
    def _(k):
        pl.semaphore_signal(
            barrier, inc=1, device_id=at(lax.rem(me + k, devices)), device_id_type=MESH)

    loads = [
        pltpu.make_async_copy(source, target, load_sem.at[i])
        for i, (source, target) in enumerate([
            (owner_in, owner_ref), (cell_in, cell_ref), (fields_in, fields_ref),
            (position_in, position_ref), (bins_in, bins_ref), (observer_in, observer_ref),
            (area_in, area_ref), (velocity_in, velocity_ref), (diffusion_in, diffusion_ref)])
    ]
    for load in loads:
        load.start()

    def request_copy(mine, other, slot_here, slot_there):
        return pltpu.make_async_remote_copy(
            src_ref=request_ref.at[mine], dst_ref=arrived_ref.at[slot_there],
            send_sem=request_send.at[mine], recv_sem=request_recv.at[slot_there],
            device_id=at(other), device_id_type=MESH)

    def sample_copy(mine, other, slot_there):
        return pltpu.make_async_remote_copy(
            src_ref=looked_ref.at[mine], dst_ref=returned_ref.at[slot_there],
            send_sem=sample_send.at[mine], recv_sem=sample_recv.at[slot_there],
            device_id=at(other), device_id_type=MESH)

    def mate_copy(source, target, send, recv, other):
        return pltpu.make_async_remote_copy(
            src_ref=source, dst_ref=target, send_sem=send, recv_sem=recv,
            device_id=member_at(my_group, other), device_id_type=MESH)

    def place_copy(other, slot):
        return mate_copy(
            place_ref.at[slot, 0:4], place_ref.at[slot, 0:4],
            place_send.at[other], place_recv.at[slot], other)

    def lines_copy(other, slot):
        return mate_copy(
            lines_out_ref.at[other], lines_ref.at[slot], lines_send.at[other], lines_recv.at[slot], other)

    def weighted_copy(other, slot):
        return mate_copy(
            weighted_ref.at[slot, 0:4], weighted_ref.at[slot, 0:4],
            weighted_send.at[other], weighted_recv.at[slot], other)

    def total_copy(i, k, other, slot):
        return pltpu.make_async_remote_copy(
            src_ref=sum_ref.at[i, k * share:(k + 1) * share], dst_ref=landed_ref.at[slot],
            send_sem=total_send.at[i * per_block + k], recv_sem=total_recv.at[slot],
            device_id=at(other), device_id_type=MESH)

    def halo_copies(stage, cells_ref, x_ref, y_out_ref, y_ref):
        def copy(k, source, target, where):
            return pltpu.make_async_remote_copy(
                src_ref=source, dst_ref=target, send_sem=halo_send.at[4 * stage + k],
                recv_sem=halo_recv.at[4 * stage + k], device_id=where, device_id_type=MESH)

        up_x, down_x = lax.rem(my_x + 1, grid_x), lax.rem(my_x + grid_x - 1, grid_x)
        up_y, down_y = lax.rem(my_y + 1, grid_y), lax.rem(my_y + grid_y - 1, grid_y)
        return [
            copy(0, cells_ref.at[:, nx - 2:nx], x_ref.at[0], (up_x, my_y)),
            copy(1, cells_ref.at[:, 0:2], x_ref.at[1], (down_x, my_y)),
            copy(2, y_out_ref.at[1], y_ref.at[0], (my_x, up_y)),
            copy(3, y_out_ref.at[0], y_ref.at[1], (my_x, down_y)),
        ]

    halo_one = halo_copies(0, fields_ref, x_one_ref, y_out_one_ref, y_one_ref)
    halo_two = halo_copies(1, middle_ref, x_two_ref, y_out_two_ref, y_two_ref)

    loads[0].wait()
    loads[1].wait()

    owner = owner_ref[...]
    cell = cell_ref[...]
    owned = (lax.broadcasted_iota(jnp.int32, (devices, panels), 0) == owner)
    owned_f = owned.astype(jnp.float32)
    owned_b = owned_f.astype(jnp.bfloat16)
    earlier = (
        lax.broadcasted_iota(jnp.int32, (128, 128), 0)
        < lax.broadcasted_iota(jnp.int32, (128, 128), 1)
    ).astype(jnp.float32).astype(jnp.bfloat16)
    running = jnp.zeros((devices, 1), jnp.float32)
    ranks = []
    for j in range(panels // 128):
        part = slice(j * 128, (j + 1) * 128)
        before = jnp.dot(owned_b[:, part], earlier, preferred_element_type=jnp.float32) + running
        ranks.append(jnp.sum(owned_f[:, part] * before, axis=0, keepdims=True))
        running = running + jnp.sum(owned_f[:, part], axis=1, keepdims=True)
    rank = jnp.concatenate(ranks, axis=1).astype(jnp.int32)
    ranked_b = (
        lax.broadcasted_iota(jnp.int32, (cap, panels), 0) == rank
    ).astype(jnp.float32).astype(jnp.bfloat16)
    ranked_ref[0:cap] = ranked_b
    ranked_ref[cap:2 * cap] = ranked_b
    cell_high = lax.shift_right_logical(cell, 7).astype(jnp.float32)
    cell_low = lax.bitwise_and(cell, 127).astype(jnp.float32)
    both = jnp.concatenate([owned_f * cell_high, owned_f * cell_low], axis=0).astype(jnp.bfloat16)
    packed = lax.dot_general(both, ranked_b, NT, preferred_element_type=jnp.float32)
    wanted = (packed[:devices] * 128.0 + packed[devices:]).astype(jnp.int32)
    for d in range(devices):
        request_ref[d] = wanted[d:d + 1]

    loads[2].wait()
    y_out_one_ref[0] = fields_ref[:, :, 0:2, :]
    y_out_one_ref[1] = fields_ref[:, :, ny - 2:ny, :]
    loads[3].wait()
    position = position_ref[...]
    place_ref[my_member, 0:1] = jnp.sum(position * position, axis=0, keepdims=True)
    place_ref[my_member, 1:4] = position
    place_ref[:, 4:5] = jnp.ones((members, 1, panels), jnp.float32)
    place_ref[:, 5:8] = jnp.zeros((members, 3, panels), jnp.float32)
    loads[4].wait()
    for j in range(members):
        for i in range(own_blocks):
            b = block_of(j, i)
            lines_out_ref[j, i:i + 1] = bins_ref[b:b + 1]
    lines_ref[my_member] = lines_out_ref[my_member]

    loads[5].wait()
    line8 = lax.broadcasted_iota(jnp.int32, (8, width), 0)
    for i in range(own_blocks):
        spot = pl.multiple_of(block_of(my_member, i) * width, width)
        o0, o1, o2 = [observer_ref[k:k + 1, pl.ds(spot, width)] for k in range(3)]
        square = o0 * o0 + o1 * o1 + o2 * o2
        near = jnp.where(line8 == 0, 1.0, 0.0)
        toward = jnp.where(line8 >= 5, -1.0, 0.0)
        for k, line in enumerate((o0, o1, o2)):
            near = jnp.where(line8 == 1 + k, -2.0 * line, near)
            toward = jnp.where(line8 == 1 + k, line, toward)
        near = jnp.where(line8 == 4, square, near)
        near_ref[i] = observer_side(near, width)
        toward_ref[i] = observer_side(toward, width)

    for c in range(quantities):
        plane = fields_ref[c].reshape(rows, depth)
        stacked = jnp.concatenate([plane[:, i * 128:(i + 1) * 128] for i in range(chunks)], axis=0)
        table_ref[c * 128:(c + 1) * 128, :] = two_parts(stacked.T, 1)

    def prepare(m):
        sides = panel_side(place_ref[m])
        depth_used = sides.shape[0]
        for i in range(own_blocks):
            left = near_ref[i][:, :depth_used]
            line = lines_ref[m, i:i + 1]
            for t in range(panels // tile):
                lanes = slice(t * tile, (t + 1) * tile)
                square = jnp.dot(left, sides[:, lanes], preferred_element_type=jnp.float32)
                inverse_ref[m, i, :, lanes] = lax.rsqrt(square)
                hot_ref[m, i, :, lanes] = (
                    lax.broadcasted_iota(jnp.int32, (bins, tile), 0) == line[:, lanes]
                ).astype(jnp.float32).astype(jnp.bfloat16)

    prepare(my_member)

    pl.semaphore_wait(barrier, devices - 1)

    @pl.loop(1, devices)
    def _(k):
        other = lax.rem(me + k, devices)
        request_copy(other, other, me, me).start()

    for copy in halo_one:
        copy.start()

    @pl.loop(1, members)
    def _(k):
        other = lax.rem(my_member + k, members)
        place_copy(other, my_member).start()
        lines_copy(other, my_member).start()

    arrived_ref[me] = request_ref[me]

    def receive_request(s):
        @pl.when(s != me)
        def _():
            request_copy(s, s, me, s).wait_recv()

    @pl.loop(0, devices // 2)
    def _(pair):
        first = lax.rem(me + devices - 2 * pair, devices)
        second = lax.rem(me + devices - 2 * pair - 1, devices)
        receive_request(first)
        receive_request(second)
        asked = jnp.concatenate([arrived_ref[first], arrived_ref[second]], axis=1)
        low = lax.bitwise_and(asked, 127)
        line = lax.shift_right_logical(asked, row_shift)
        chunk = lax.bitwise_and(lax.shift_right_logical(asked, 7), chunks - 1)
        high = chunk * rows + line
        pick = (
            lax.broadcasted_iota(jnp.int32, (chunks * rows, 2 * cap), 0) == high
        ).astype(jnp.float32).astype(jnp.bfloat16)
        found = jnp.dot(
            table_ref[...], jnp.concatenate([pick, pick], axis=0),
            preferred_element_type=jnp.float32)
        lane = lax.broadcasted_iota(jnp.int32, (128, 2 * cap), 0) == low
        values = jnp.concatenate(
            [
                jnp.sum(jnp.where(lane, found[c * 128:(c + 1) * 128], 0.0), axis=0, keepdims=True)
                for c in range(quantities)
            ],
            axis=0,
        )
        looked_ref[first] = values[:, :cap]
        looked_ref[second] = values[:, cap:]

        @pl.when(first != me)
        def _():
            sample_copy(first, first, me).start()

        sample_copy(second, second, me).start()

    returned_ref[me] = looked_ref[me]

    @pl.loop(1, members)
    def _(k):
        m = lax.rem(my_member + members - k, members)
        place_copy(m, m).wait_recv()
        lines_copy(m, m).wait_recv()
        prepare(m)

    for load in loads[6:]:
        load.wait()
    for copy in halo_one:
        copy.wait_recv()

    def keep_middle(c, x, center, rate):
        value = center + time_step * rate
        middle_ref[c, x] = value
        y_out_two_ref[0, c, x] = value[0:2]
        y_out_two_ref[1, c, x] = value[ny - 2:ny]

    section(fields_ref, x_one_ref, y_one_ref, pad_ref, velocity_ref, diffusion_ref, keep_middle)
    for copy in halo_two:
        copy.start()

    @pl.loop(1, devices)
    def _(k):
        s = lax.rem(me + devices - k, devices)
        sample_copy(s, s, s).wait_recv()

    got = jnp.concatenate([returned_ref[d] for d in range(devices)], axis=0)
    spread = jnp.dot(two_parts(got, 1), ranked_ref[...], preferred_element_type=jnp.float32)
    named = lax.broadcasted_iota(jnp.int32, (devices * quantities, panels), 0) // quantities
    kept = jnp.where(named == owner_ref[...], spread, 0.0)
    pair = kept[0:2 * quantities]
    for a in range(1, devices // 2):
        pair = pair + kept[2 * quantities * a:2 * quantities * (a + 1)]
    weighted_ref[my_member, 0:4] = (pair[:quantities] + pair[quantities:]) * (scale * area_ref[...])

    @pl.loop(1, members)
    def _(k):
        weighted_copy(lax.rem(my_member + k, members), my_member).start()

    sum_ref[...] = jnp.zeros(sum_ref.shape, jnp.float32)

    def contribute(m):
        mine = weighted_ref[m, 0:4]
        weighted_ref[m, 4:8] = mine * place_ref[m, 0:4]
        sides = panel_side(weighted_ref[m])
        depth_used = sides.shape[0]
        for i in range(own_blocks):
            left = toward_ref[i][:, :depth_used]
            acc = sum_ref[i]
            for t in range(panels // tile):
                lanes = slice(t * tile, (t + 1) * tile)
                along = jnp.dot(left, sides[:, lanes], preferred_element_type=jnp.float32)
                inverse = inverse_ref[m, i, :, lanes]
                emitted = ((mine[0:1, lanes] + along * inverse) * inverse).astype(jnp.bfloat16)
                acc = acc + lax.dot_general(
                    emitted, hot_ref[m, i, :, lanes], NT, preferred_element_type=jnp.float32)
            sum_ref[i] = acc

    contribute(my_member)

    @pl.loop(1, members)
    def _(k):
        m = lax.rem(my_member + members - k, members)
        weighted_copy(m, m).wait_recv()
        contribute(m)

    for i in range(own_blocks):
        for k in range(per_block):
            target = block_of(my_member, i) * per_block + k

            @pl.when(target != me)
            def _():
                total_copy(i, k, target, my_group).start()

            @pl.when(target == me)
            def _():
                landed_ref[my_group] = sum_ref[i, k * share:(k + 1) * share]

    for copy in halo_two:
        copy.wait_recv()

    def keep_advanced(c, x, center, rate):
        advanced_ref[c, x] = 0.5 * fields_ref[c, x] + 0.5 * (center + time_step * rate)

    section(middle_ref, x_two_ref, y_two_ref, pad_ref, velocity_ref, diffusion_ref, keep_advanced)

    @pl.loop(1, devices)
    def _(k):
        other = lax.rem(me + k, devices)
        request_copy(other, other, me, me).wait_send()
        sample_copy(other, other, me).wait_send()

    @pl.loop(1, members)
    def _(k):
        other = lax.rem(my_member + k, members)
        place_copy(other, my_member).wait_send()
        lines_copy(other, my_member).wait_send()
        weighted_copy(other, my_member).wait_send()

    for copy in halo_one + halo_two:
        copy.wait_send()

    for i in range(own_blocks):
        for k in range(per_block):
            target = block_of(my_member, i) * per_block + k

            @pl.when(target != me)
            def _():
                total_copy(i, k, target, my_group).wait_send()

    source = member_of(me // per_block)

    @pl.loop(0, groups)
    def _(g):
        @pl.when(jnp.logical_or(g != my_group, source != my_member))
        def _():
            total_copy(0, 0, lax.rem(me + 1, devices), g).wait_recv()

    signal_ref[...] = jnp.sum(landed_ref[...], axis=0)


def per_device(
    bins, fields, velocity, diffusion, panel_owner, panel_cell, panel_bins,
    panel_position, panel_area, observer_position,
):
    grid_x = lax.axis_size("gx")
    grid_y = lax.axis_size("gy")
    devices = grid_x * grid_y
    panels = panel_cell.shape[0]
    cap = 4 * panels // devices
    blocks = panel_bins.shape[0]
    observers = observer_position.shape[1]
    share = observers // devices
    width = observers // blocks
    quantities = fields.shape[0]
    scale = (bins / (panels * devices)) ** 0.5
    columns = 2 * fields.shape[1] * fields.shape[2] * fields.shape[3] // 128
    members = 2 * grid_y
    own_blocks = blocks // members
    sends = own_blocks * (width // share)

    owner, cell, area = (
        panel_owner.reshape(1, panels), panel_cell.reshape(1, panels), panel_area.reshape(1, panels))
    vmem = pl.BlockSpec(memory_space=pltpu.VMEM)
    anywhere = pl.BlockSpec(memory_space=pl.ANY)
    nx, ny, nz = fields.shape[1:]
    beside_x = pltpu.VMEM((2, quantities, 2, ny, nz), jnp.float32)
    beside_y = pltpu.VMEM((2, quantities, nx, 2, nz), jnp.float32)
    return pl.pallas_call(
        functools.partial(emission_kernel, grid_x, grid_y, cap, scale, min(256, panels)),
        out_shape=(
            jax.ShapeDtypeStruct(fields.shape, jnp.float32),
            jax.ShapeDtypeStruct((share, bins), jnp.float32),
        ),
        in_specs=[anywhere] * 9,
        out_specs=(vmem, vmem),
        scratch_shapes=[
            pltpu.VMEM(fields.shape, jnp.float32),
            pltpu.VMEM(velocity.shape, jnp.float32),
            pltpu.SMEM(diffusion.shape, jnp.float32),
        ] + [
            pltpu.VMEM(array.shape, array.dtype)
            for array in (owner, cell, panel_bins, panel_position, area, observer_position)
        ] + [
            pltpu.VMEM(fields.shape, jnp.float32),
            pltpu.VMEM((quantities, nx, ny + 16, nz), jnp.float32),
            beside_x, beside_x, beside_y, beside_y, beside_y, beside_y,
            pltpu.VMEM((devices, 1, cap), jnp.int32),
            pltpu.VMEM((devices, 1, cap), jnp.int32),
            pltpu.VMEM((devices, quantities, cap), jnp.float32),
            pltpu.VMEM((devices, quantities, cap), jnp.float32),
            pltpu.VMEM((quantities * 128, columns), jnp.bfloat16),
            pltpu.VMEM((2 * cap, panels), jnp.bfloat16),
            pltpu.VMEM((members, 8, panels), jnp.float32),
            pltpu.VMEM((members, own_blocks, panels), jnp.int32),
            pltpu.VMEM((members, own_blocks, panels), jnp.int32),
            pltpu.VMEM((members, 8, panels), jnp.float32),
            pltpu.VMEM((own_blocks, width, 128), jnp.bfloat16),
            pltpu.VMEM((own_blocks, width, 128), jnp.bfloat16),
            pltpu.VMEM((members, own_blocks, width, panels), jnp.float32),
            pltpu.VMEM((members, own_blocks, bins, panels), jnp.bfloat16),
            pltpu.VMEM((own_blocks, width, bins), jnp.float32),
            pltpu.VMEM((devices // members, share, bins), jnp.float32),
        ] + [
            pltpu.SemaphoreType.DMA((devices,))] * 4 + [
            pltpu.SemaphoreType.DMA((sends,)),
            pltpu.SemaphoreType.DMA((devices // members,))] + [
            pltpu.SemaphoreType.DMA((8,))] * 2 + [
            pltpu.SemaphoreType.DMA((members,))] * 6 + [
            pltpu.SemaphoreType.DMA((9,))],
        compiler_params=pltpu.CompilerParams(
            collective_id=0, has_side_effects=True),
        cost_estimate=pl.CostEstimate(
            flops=40 * 10**9, bytes_accessed=4 * 10**6, transcendentals=2 * 10**6),
    )(fields, velocity, diffusion, owner, cell, panel_bins, panel_position, area, observer_position)


def solution(mesh):
    in_specs = (
        P(None, "gx", "gy", None),
        P(None, "gx", "gy", None),
        P(),
        P(("gx", "gy"), None),
        P(("gx", "gy")),
        P(None, ("gx", "gy")),
        P(None, ("gx", "gy")),
        P(("gx", "gy")),
        P(),
    )
    out_specs = (P(None, "gx", "gy", None), P(("gx", "gy"), None))
    return jax.shard_map(
        functools.partial(per_device, 128),
        mesh=mesh, in_specs=in_specs, out_specs=out_specs, check_vma=False,
    )
```

```python
import functools

import jax
import jax.numpy as jnp
from jax import lax
from jax.experimental import pallas as pl
from jax.experimental.pallas import tpu as pltpu
from jax.sharding import PartitionSpec as P

MESH = pl.DeviceIdType.MESH
time_step = 0.15
NT = (((1,), (1,)), ((), ()))


def axis_terms(center, ahead_one, ahead_two, behind_one, behind_two):
    first = (8.0 * (ahead_one - behind_one) - (ahead_two - behind_two)) / 12.0
    second = (16.0 * (ahead_one + behind_one) - (ahead_two + behind_two) - 30.0 * center) / 12.0
    return (first, second)


def section(cells_ref, x_ref, y_ref, pad_ref, velocity_ref, diffusion_ref, write):
    quantities, nx, ny, nz = cells_ref.shape
    for c in range(quantities):
        def plane(x):
            if x < 0:
                return x_ref[0, c, 2 + x]
            if x >= nx:
                return x_ref[1, c, x - nx]
            return cells_ref[c, x]

        for x in range(nx):
            center = cells_ref[c, x]
            pad_ref[c, x, 6:8, :] = y_ref[0, c, x]
            pad_ref[c, x, 8:8 + ny, :] = center
            pad_ref[c, x, 8 + ny:10 + ny, :] = y_ref[1, c, x]

            def along_y(k):
                return pad_ref[c, x, 8 + k:8 + k + ny, :]

            first_x, second_x = axis_terms(
                center, plane(x + 1), plane(x + 2), plane(x - 1), plane(x - 2))
            first_y, second_y = axis_terms(
                center, along_y(1), along_y(2), along_y(-1), along_y(-2))
            first_z, second_z = axis_terms(
                center, pltpu.roll(center, nz - 1, 1), pltpu.roll(center, nz - 2, 1),
                pltpu.roll(center, 1, 1), pltpu.roll(center, 2, 1))
            advect = (
                velocity_ref[0, x] * first_x + velocity_ref[1, x] * first_y
                + velocity_ref[2, x] * first_z)
            write(c, x, center, -advect + diffusion_ref[c] * (second_x + second_y + second_z))


def two_parts(values, axis):
    high = values.astype(jnp.bfloat16)
    low = (values - high.astype(jnp.float32)).astype(jnp.bfloat16)
    return jnp.concatenate([high, low], axis=axis)


def three_parts(values):
    high = values.astype(jnp.bfloat16).astype(jnp.float32)
    rest = values - high
    middle = rest.astype(jnp.bfloat16).astype(jnp.float32)
    return high, middle, rest - middle


def observer_side(values, width):
    high, middle, low = three_parts(values)
    pieces = [high, middle, low, high, middle, high]
    used = len(pieces) * values.shape[0]
    filled = jnp.concatenate(pieces + [jnp.zeros((128 - used, width), jnp.float32)], axis=0)
    return filled.T.astype(jnp.bfloat16)


def panel_side(values):
    high, middle, low = three_parts(values)
    return jnp.concatenate([high, high, high, middle, middle, low], axis=0).astype(jnp.bfloat16)


def emission_kernel(
    grid_x, grid_y, cap, scale, tile,
    fields_in, velocity_in, diffusion_in, owner_in, cell_in, bins_in, position_in, area_in, observer_in,
    advanced_ref, signal_ref,
    fields_ref, velocity_ref, diffusion_ref, owner_ref, cell_ref, bins_ref, position_ref, area_ref, observer_ref,
    middle_ref, pad_ref, x_one_ref, x_two_ref, y_one_ref, y_two_ref, y_out_one_ref, y_out_two_ref,
    request_ref, arrived_ref, looked_ref, returned_ref, table_ref, ranked_ref,
    place_ref, lines_out_ref, lines_ref, weighted_ref, near_ref, toward_ref, inverse_ref, hot_ref, sum_ref, landed_ref,
    request_send, request_recv, sample_send, sample_recv, total_send, total_recv,
    halo_send, halo_recv, place_send, place_recv, lines_send, lines_recv, weighted_send, weighted_recv, load_sem,
):
    devices = grid_x * grid_y
    my_x, my_y = lax.axis_index("gx"), lax.axis_index("gy")
    me = my_x * grid_y + my_y
    nx, ny = fields_ref.shape[1:3]
    panels = owner_ref.shape[1]
    blocks, bins = bins_ref.shape[0], signal_ref.shape[1]
    observers = observer_ref.shape[1]
    width = observers // blocks
    share = observers // devices
    per_block = width // share
    quantities = fields_ref.shape[0]
    rows = fields_ref.shape[1] * fields_ref.shape[2]
    depth = fields_ref.shape[3]
    chunks = depth // 128
    row_shift = (depth - 1).bit_length()

    members = 2 * grid_y
    groups = devices // members
    own_blocks = blocks // members
    across = grid_y // 2
    my_bit = lax.rem(my_x // 2, 2)
    my_member = my_bit * grid_y + my_y
    my_group = (my_x // 4) * 2 + lax.rem(my_x, 2)

    def at(d):
        return (d // grid_y, lax.rem(d, grid_y))

    def member_at(group, member):
        x = (group // 2) * 4 + (member // grid_y) * 2 + lax.rem(group, 2)
        return (x, lax.rem(member, grid_y))

    def block_of(member, i):
        bit, y = member // grid_y, member % grid_y
        return ((y % 2) * 2 + bit) * (own_blocks * across) + i * across + y // 2

    def member_of(block):
        y = lax.rem(block, across)
        bit = lax.rem(block // (across * own_blocks), 2)
        core = block // (across * own_blocks * 2)
        return bit * grid_y + y * 2 + core

    device_bits = [1 << b for b in range((devices - 1).bit_length())]
    device_steps = [bit * (1 - 2 * lax.rem(me // bit, 2)) for bit in device_bits]

    def peer(k):
        return me + sum(step for bit, step in zip(device_bits, device_steps) if k & bit)

    def flipped(base, k, bits):
        for bit in bits:
            base = base + bit * lax.rem(k // bit, 2) * (1 - 2 * lax.rem(base // bit, 2))
        return base

    member_bits = [1 << b for b in range((members - 1).bit_length())]

    def mate(k):
        return flipped(my_member, k, member_bits)

    barrier = pltpu.get_barrier_semaphore()

    for k in reversed(range(1, devices)):
        pl.semaphore_signal(barrier, inc=1, device_id=at(peer(k)), device_id_type=MESH)

    loads = [
        pltpu.make_async_copy(source, target, load_sem.at[i])
        for i, (source, target) in enumerate([
            (owner_in, owner_ref), (cell_in, cell_ref), (fields_in, fields_ref),
            (position_in, position_ref), (bins_in, bins_ref), (observer_in, observer_ref),
            (area_in, area_ref), (velocity_in, velocity_ref), (diffusion_in, diffusion_ref)])
    ]
    for load in loads:
        load.start()

    def request_copy(mine, other, slot_here, slot_there):
        return pltpu.make_async_remote_copy(
            src_ref=request_ref.at[mine], dst_ref=arrived_ref.at[slot_there],
            send_sem=request_send.at[mine], recv_sem=request_recv.at[slot_there],
            device_id=at(other), device_id_type=MESH)

    def sample_copy(mine, other, slot_there):
        return pltpu.make_async_remote_copy(
            src_ref=looked_ref.at[mine], dst_ref=returned_ref.at[slot_there],
            send_sem=sample_send.at[mine], recv_sem=sample_recv.at[slot_there],
            device_id=at(other), device_id_type=MESH)

    def mate_copy(source, target, send, recv, other):
        return pltpu.make_async_remote_copy(
            src_ref=source, dst_ref=target, send_sem=send, recv_sem=recv,
            device_id=member_at(my_group, other), device_id_type=MESH)

    def place_copy(other, slot):
        return mate_copy(
            place_ref.at[slot, 0:4], place_ref.at[slot, 0:4],
            place_send.at[other], place_recv.at[slot], other)

    def lines_copy(other, slot):
        return mate_copy(
            lines_out_ref.at[other], lines_ref.at[slot], lines_send.at[other], lines_recv.at[slot], other)

    def weighted_copy(other, slot):
        return mate_copy(
            weighted_ref.at[slot, 0:4], weighted_ref.at[slot, 0:4],
            weighted_send.at[other], weighted_recv.at[slot], other)

    def total_copy(i, k, other, slot):
        return pltpu.make_async_remote_copy(
            src_ref=sum_ref.at[i, k * share:(k + 1) * share], dst_ref=landed_ref.at[slot],
            send_sem=total_send.at[i * per_block + k], recv_sem=total_recv.at[slot],
            device_id=at(other), device_id_type=MESH)

    def halo_copies(stage, cells_ref, x_ref, y_out_ref, y_ref):
        def copy(k, source, target, where):
            return pltpu.make_async_remote_copy(
                src_ref=source, dst_ref=target, send_sem=halo_send.at[4 * stage + k],
                recv_sem=halo_recv.at[4 * stage + k], device_id=where, device_id_type=MESH)

        up_x, down_x = lax.rem(my_x + 1, grid_x), lax.rem(my_x + grid_x - 1, grid_x)
        up_y, down_y = lax.rem(my_y + 1, grid_y), lax.rem(my_y + grid_y - 1, grid_y)
        return [
            copy(0, cells_ref.at[:, nx - 2:nx], x_ref.at[0], (up_x, my_y)),
            copy(1, cells_ref.at[:, 0:2], x_ref.at[1], (down_x, my_y)),
            copy(2, y_out_ref.at[1], y_ref.at[0], (my_x, up_y)),
            copy(3, y_out_ref.at[0], y_ref.at[1], (my_x, down_y)),
        ]

    halo_one = halo_copies(0, fields_ref, x_one_ref, y_out_one_ref, y_one_ref)
    halo_two = halo_copies(1, middle_ref, x_two_ref, y_out_two_ref, y_two_ref)

    loads[0].wait()
    loads[1].wait()

    owner = owner_ref[...]
    cell = cell_ref[...]
    owned = (lax.broadcasted_iota(jnp.int32, (devices, panels), 0) == owner)
    owned_f = owned.astype(jnp.float32)
    owned_b = owned_f.astype(jnp.bfloat16)
    earlier = (
        lax.broadcasted_iota(jnp.int32, (128, 128), 0)
        < lax.broadcasted_iota(jnp.int32, (128, 128), 1)
    ).astype(jnp.float32).astype(jnp.bfloat16)
    running = jnp.zeros((devices, 1), jnp.float32)
    ranks = []
    for j in range(panels // 128):
        part = slice(j * 128, (j + 1) * 128)
        before = jnp.dot(owned_b[:, part], earlier, preferred_element_type=jnp.float32) + running
        ranks.append(jnp.sum(owned_f[:, part] * before, axis=0, keepdims=True))
        running = running + jnp.sum(owned_f[:, part], axis=1, keepdims=True)
    rank = jnp.concatenate(ranks, axis=1).astype(jnp.int32)
    ranked_b = (
        lax.broadcasted_iota(jnp.int32, (cap, panels), 0) == rank
    ).astype(jnp.float32).astype(jnp.bfloat16)
    ranked_ref[0:cap] = ranked_b
    ranked_ref[cap:2 * cap] = ranked_b
    cell_high = lax.shift_right_logical(cell, 7).astype(jnp.float32)
    cell_low = lax.bitwise_and(cell, 127).astype(jnp.float32)
    both = jnp.concatenate([owned_f * cell_high, owned_f * cell_low], axis=0).astype(jnp.bfloat16)
    packed = lax.dot_general(both, ranked_b, NT, preferred_element_type=jnp.float32)
    wanted = (packed[:devices] * 128.0 + packed[devices:]).astype(jnp.int32)
    for d in range(devices):
        request_ref[d] = wanted[d:d + 1]

    loads[2].wait()
    y_out_one_ref[0] = fields_ref[:, :, 0:2, :]
    y_out_one_ref[1] = fields_ref[:, :, ny - 2:ny, :]
    loads[3].wait()
    position = position_ref[...]
    place_ref[my_member, 0:1] = jnp.sum(position * position, axis=0, keepdims=True)
    place_ref[my_member, 1:4] = position
    place_ref[:, 4:5] = jnp.ones((members, 1, panels), jnp.float32)
    place_ref[:, 5:8] = jnp.zeros((members, 3, panels), jnp.float32)
    loads[4].wait()
    for j in range(members):
        for i in range(own_blocks):
            b = block_of(j, i)
            lines_out_ref[j, i:i + 1] = bins_ref[b:b + 1]
    lines_ref[my_member] = lines_out_ref[my_member]

    loads[5].wait()
    line8 = lax.broadcasted_iota(jnp.int32, (8, width), 0)
    for i in range(own_blocks):
        spot = pl.multiple_of(block_of(my_member, i) * width, width)
        o0, o1, o2 = [observer_ref[k:k + 1, pl.ds(spot, width)] for k in range(3)]
        square = o0 * o0 + o1 * o1 + o2 * o2
        near = jnp.where(line8 == 0, 1.0, 0.0)
        toward = jnp.where(line8 >= 5, -1.0, 0.0)
        for k, line in enumerate((o0, o1, o2)):
            near = jnp.where(line8 == 1 + k, -2.0 * line, near)
            toward = jnp.where(line8 == 1 + k, line, toward)
        near = jnp.where(line8 == 4, square, near)
        near_ref[i] = observer_side(near, width)
        toward_ref[i] = observer_side(toward, width)

    for c in range(quantities):
        plane = fields_ref[c].reshape(rows, depth)
        stacked = jnp.concatenate([plane[:, i * 128:(i + 1) * 128] for i in range(chunks)], axis=0)
        table_ref[c * 128:(c + 1) * 128, :] = two_parts(stacked.T, 1)

    def prepare(m):
        sides = panel_side(place_ref[m])
        depth_used = sides.shape[0]
        for i in range(own_blocks):
            left = near_ref[i][:, :depth_used]
            line = lines_ref[m, i:i + 1]
            for t in range(panels // tile):
                lanes = slice(t * tile, (t + 1) * tile)
                square = jnp.dot(left, sides[:, lanes], preferred_element_type=jnp.float32)
                inverse_ref[m, i, :, lanes] = lax.rsqrt(square)
                hot_ref[m, i, :, lanes] = (
                    lax.broadcasted_iota(jnp.int32, (bins, tile), 0) == line[:, lanes]
                ).astype(jnp.float32).astype(jnp.bfloat16)

    prepare(my_member)

    pl.semaphore_wait(barrier, devices - 1)

    for k in reversed(range(1, devices)):
        other = peer(k)
        request_copy(other, other, me, me).start()

    @pl.loop(1, members)
    def _(k):
        other = mate(k)
        place_copy(other, my_member).start()
        lines_copy(other, my_member).start()

    for copy in halo_one:
        copy.start()

    arrived_ref[me] = request_ref[me]

    def prepare_mates(first, last):
        @pl.loop(first, last)
        def _(k):
            m = mate(k)
            place_copy(m, m).wait_recv()
            lines_copy(m, m).wait_recv()
            prepare(m)

    early = members // 2
    prepare_mates(1, early)

    def receive_request(s):
        @pl.when(s != me)
        def _():
            request_copy(s, s, me, s).wait_recv()

    batch = min(8, devices)

    @pl.loop(0, devices // batch)
    def _(turn):
        base = flipped(me, turn * batch, device_bits)
        sources = [flipped(base, k, device_bits) for k in range(batch)]
        for s in sources:
            receive_request(s)
        asked = jnp.concatenate([arrived_ref[s] for s in sources], axis=1)
        low = lax.bitwise_and(asked, 127)
        line = lax.shift_right_logical(asked, row_shift)
        chunk = lax.bitwise_and(lax.shift_right_logical(asked, 7), chunks - 1)
        high = chunk * rows + line
        span = batch * cap
        step = min(256, span)
        for first in range(0, span, step):
            part = slice(first, first + step)
            pick = (
                lax.broadcasted_iota(jnp.int32, (chunks * rows, step), 0) == high[:, part]
            ).astype(jnp.float32).astype(jnp.bfloat16)
            found = jnp.dot(
                table_ref[...], jnp.concatenate([pick, pick], axis=0),
                preferred_element_type=jnp.float32)
            lane = lax.broadcasted_iota(jnp.int32, (128, step), 0) == low[:, part]
            values = jnp.concatenate(
                [
                    jnp.sum(
                        jnp.where(lane, found[c * 128:(c + 1) * 128], 0.0), axis=0, keepdims=True)
                    for c in range(quantities)
                ],
                axis=0,
            )
            for k in range(step // cap):
                looked_ref[sources[first // cap + k]] = values[:, k * cap:(k + 1) * cap]

        for s in sources:
            @pl.when(s != me)
            def _():
                sample_copy(s, s, me).start()

    returned_ref[me] = looked_ref[me]

    for load in loads[6:]:
        load.wait()
    for copy in halo_one:
        copy.wait_recv()

    def keep_middle(c, x, center, rate):
        value = center + time_step * rate
        middle_ref[c, x] = value
        y_out_two_ref[0, c, x] = value[0:2]
        y_out_two_ref[1, c, x] = value[ny - 2:ny]

    section(fields_ref, x_one_ref, y_one_ref, pad_ref, velocity_ref, diffusion_ref, keep_middle)
    for copy in halo_two:
        copy.start()

    prepare_mates(early, members)

    @pl.loop(1, devices)
    def _(k):
        s = lax.rem(me + devices - k, devices)
        sample_copy(s, s, s).wait_recv()

    got = jnp.concatenate([returned_ref[d] for d in range(devices)], axis=0)
    spread = jnp.dot(two_parts(got, 1), ranked_ref[...], preferred_element_type=jnp.float32)
    named = lax.broadcasted_iota(jnp.int32, (devices * quantities, panels), 0) // quantities
    kept = jnp.where(named == owner_ref[...], spread, 0.0)
    pair = kept[0:2 * quantities]
    for a in range(1, devices // 2):
        pair = pair + kept[2 * quantities * a:2 * quantities * (a + 1)]
    weighted_ref[my_member, 0:4] = (pair[:quantities] + pair[quantities:]) * (scale * area_ref[...])

    @pl.loop(1, members)
    def _(k):
        weighted_copy(mate(members - k), my_member).start()

    sum_ref[...] = jnp.zeros(sum_ref.shape, jnp.float32)

    def contribute(m):
        mine = weighted_ref[m, 0:4]
        weighted_ref[m, 4:8] = mine * place_ref[m, 0:4]
        sides = panel_side(weighted_ref[m])
        depth_used = sides.shape[0]
        for i in range(own_blocks):
            left = toward_ref[i][:, :depth_used]
            acc = sum_ref[i]
            for t in range(panels // tile):
                lanes = slice(t * tile, (t + 1) * tile)
                along = jnp.dot(left, sides[:, lanes], preferred_element_type=jnp.float32)
                inverse = inverse_ref[m, i, :, lanes]
                emitted = ((mine[0:1, lanes] + along * inverse) * inverse).astype(jnp.bfloat16)
                acc = acc + lax.dot_general(
                    emitted, hot_ref[m, i, :, lanes], NT, preferred_element_type=jnp.float32)
            sum_ref[i] = acc

    contribute(my_member)

    @pl.loop(1, members)
    def _(k):
        m = mate(k)
        weighted_copy(m, m).wait_recv()
        contribute(m)

    for i in range(own_blocks):
        for k in range(per_block):
            target = block_of(my_member, i) * per_block + k

            @pl.when(target != me)
            def _():
                total_copy(i, k, target, my_group).start()

            @pl.when(target == me)
            def _():
                landed_ref[my_group] = sum_ref[i, k * share:(k + 1) * share]

    for copy in halo_two:
        copy.wait_recv()

    def keep_advanced(c, x, center, rate):
        advanced_ref[c, x] = 0.5 * fields_ref[c, x] + 0.5 * (center + time_step * rate)

    section(middle_ref, x_two_ref, y_two_ref, pad_ref, velocity_ref, diffusion_ref, keep_advanced)

    @pl.loop(1, devices)
    def _(k):
        other = lax.rem(me + k, devices)
        request_copy(other, other, me, me).wait_send()
        sample_copy(other, other, me).wait_send()

    @pl.loop(1, members)
    def _(k):
        other = mate(k)
        place_copy(other, my_member).wait_send()
        lines_copy(other, my_member).wait_send()
        weighted_copy(other, my_member).wait_send()

    for copy in halo_one + halo_two:
        copy.wait_send()

    for i in range(own_blocks):
        for k in range(per_block):
            target = block_of(my_member, i) * per_block + k

            @pl.when(target != me)
            def _():
                total_copy(i, k, target, my_group).wait_send()

    source = member_of(me // per_block)

    @pl.loop(0, groups)
    def _(g):
        @pl.when(jnp.logical_or(g != my_group, source != my_member))
        def _():
            total_copy(0, 0, lax.rem(me + 1, devices), g).wait_recv()

    signal_ref[...] = jnp.sum(landed_ref[...], axis=0)


def write_kernel(advanced_in, signal_in, advanced_out, signal_out, sems):
    copies = [
        pltpu.make_async_copy(advanced_in, advanced_out, sems.at[0]),
        pltpu.make_async_copy(signal_in, signal_out, sems.at[1]),
    ]
    for copy in copies:
        copy.start()
    for copy in copies:
        copy.wait()


def per_device(
    bins, fields, velocity, diffusion, panel_owner, panel_cell, panel_bins,
    panel_position, panel_area, observer_position,
):
    grid_x = lax.axis_size("gx")
    grid_y = lax.axis_size("gy")
    devices = grid_x * grid_y
    panels = panel_cell.shape[0]
    cap = 4 * panels // devices
    blocks = panel_bins.shape[0]
    observers = observer_position.shape[1]
    share = observers // devices
    width = observers // blocks
    quantities = fields.shape[0]
    scale = (bins / (panels * devices)) ** 0.5
    columns = 2 * fields.shape[1] * fields.shape[2] * fields.shape[3] // 128
    members = 2 * grid_y
    own_blocks = blocks // members
    sends = own_blocks * (width // share)

    owner, cell, area = (
        panel_owner.reshape(1, panels), panel_cell.reshape(1, panels), panel_area.reshape(1, panels))
    vmem = pl.BlockSpec(memory_space=pltpu.VMEM)
    anywhere = pl.BlockSpec(memory_space=pl.ANY)
    outside = pl.BlockSpec(memory_space=pltpu.HBM)
    nx, ny, nz = fields.shape[1:]
    beside_x = pltpu.VMEM((2, quantities, 2, ny, nz), jnp.float32)
    beside_y = pltpu.VMEM((2, quantities, nx, 2, nz), jnp.float32)
    held = pl.pallas_call(
        functools.partial(emission_kernel, grid_x, grid_y, cap, scale, min(256, panels)),
        out_shape=(
            pltpu.VMEM(fields.shape, jnp.float32),
            pltpu.VMEM((share, bins), jnp.float32),
        ),
        in_specs=[outside] * 9,
        out_specs=(vmem, vmem),
        scratch_shapes=[
            pltpu.VMEM(fields.shape, jnp.float32),
            pltpu.VMEM(velocity.shape, jnp.float32),
            pltpu.SMEM(diffusion.shape, jnp.float32),
        ] + [
            pltpu.VMEM(array.shape, array.dtype)
            for array in (owner, cell, panel_bins, panel_position, area, observer_position)
        ] + [
            pltpu.VMEM(fields.shape, jnp.float32),
            pltpu.VMEM((quantities, nx, ny + 16, nz), jnp.float32),
            beside_x, beside_x, beside_y, beside_y, beside_y, beside_y,
            pltpu.VMEM((devices, 1, cap), jnp.int32),
            pltpu.VMEM((devices, 1, cap), jnp.int32),
            pltpu.VMEM((devices, quantities, cap), jnp.float32),
            pltpu.VMEM((devices, quantities, cap), jnp.float32),
            pltpu.VMEM((quantities * 128, columns), jnp.bfloat16),
            pltpu.VMEM((2 * cap, panels), jnp.bfloat16),
            pltpu.VMEM((members, 8, panels), jnp.float32),
            pltpu.VMEM((members, own_blocks, panels), jnp.int32),
            pltpu.VMEM((members, own_blocks, panels), jnp.int32),
            pltpu.VMEM((members, 8, panels), jnp.float32),
            pltpu.VMEM((own_blocks, width, 128), jnp.bfloat16),
            pltpu.VMEM((own_blocks, width, 128), jnp.bfloat16),
            pltpu.VMEM((members, own_blocks, width, panels), jnp.float32),
            pltpu.VMEM((members, own_blocks, bins, panels), jnp.bfloat16),
            pltpu.VMEM((own_blocks, width, bins), jnp.float32),
            pltpu.VMEM((devices // members, share, bins), jnp.float32),
        ] + [
            pltpu.SemaphoreType.DMA((devices,))] * 4 + [
            pltpu.SemaphoreType.DMA((sends,)),
            pltpu.SemaphoreType.DMA((devices // members,))] + [
            pltpu.SemaphoreType.DMA((8,))] * 2 + [
            pltpu.SemaphoreType.DMA((members,))] * 6 + [
            pltpu.SemaphoreType.DMA((9,))],
        compiler_params=pltpu.CompilerParams(
            collective_id=0, has_side_effects=True),
        cost_estimate=pl.CostEstimate(
            flops=40 * 10**9, bytes_accessed=4 * 10**6, transcendentals=2 * 10**6),
    )(fields, velocity, diffusion, owner, cell, panel_bins, panel_position, area, observer_position)
    return pl.pallas_call(
        write_kernel,
        out_shape=(
            jax.ShapeDtypeStruct(fields.shape, jnp.float32),
            jax.ShapeDtypeStruct((share, bins), jnp.float32),
        ),
        in_specs=[anywhere, anywhere],
        out_specs=(outside, outside),
        scratch_shapes=[pltpu.SemaphoreType.DMA((2,))],
        compiler_params=pltpu.CompilerParams(vmem_limit_bytes=2**20),
    )(*held)


def solution(mesh):
    in_specs = (
        P(None, "gx", "gy", None),
        P(None, "gx", "gy", None),
        P(),
        P(("gx", "gy"), None),
        P(("gx", "gy")),
        P(None, ("gx", "gy")),
        P(None, ("gx", "gy")),
        P(("gx", "gy")),
        P(),
    )
    out_specs = (P(None, "gx", "gy", None), P(("gx", "gy"), None))
    return jax.shard_map(
        functools.partial(per_device, 128),
        mesh=mesh, in_specs=in_specs, out_specs=out_specs, check_vma=False,
    )
```
